32 devices in a mesh: groups: 2 (over y), space: 4 (over x, core), tm: 4 (over z).
Axes of the slice: x: 2, y: 2, z: 4, core: 2. Of those that a mesh axis runs over, the one named last changes fastest.
Arguments:
- couplings: float32 [9, 4, 4, 2, 4, 96, 192], P(None, 'tm', 'space'), may hold values from -0.15625 to 0.15625
- source: float32 [4, 4, 2, 4, 96, 256], P('tm', 'space'), may hold values from -6 to 6
- initial: float32 [4, 4, 2, 4, 96, 256], P('tm', 'space'), may hold values from -6 to 6
- vectors: float32 [512, 4, 4, 2, 4, 192], P(None, 'tm', 'space'), may hold values from -0.0390625 to 0.0390625
- inverse_eigen: float32 [2, 512], replicated, may hold values from -20 to 20
Outputs:
- solution: float32 [8, 4, 2, 4, 96, 256], P(('groups', 'tm'), 'space'), parts along dimension 0
- residual: float32 [8, 4, 2, 4, 96, 256], P(('groups', 'tm'), 'space'), parts along dimension 0
The draws below stay inside these ranges and needn't reach their ends.
There are 2 independent parts, one for each index of `groups`. The reference program is written for one: setup_inputs(seed, part) draws one part's arguments, and reference() takes and returns one part's arrays. A program takes and returns all parts, laid end to end along the dimension named above; an argument that names none is the same for every part. Nothing has to cross between parts.
All inputs are finite; a program needn't handle non-finite values.
Results may differ from the reference program's by a relative error of at most 0.0001.
Values sent between devices are 32-bit elements; how exact they have to be, the bound alone decides.
A program may use at most 64 MiB of HBM per device.

```python
import jax
import jax.numpy as jnp
from jax import lax

NC = 96
NR = 128
NV = 512
LX = 4
LY = 2
ITERS = 2
NZ = 4
NT = 4


def block_scale(rng, shape, cuts, smallest, top_value):
    level, own = 1.0, jax.random.fold_in(rng, 6)
    for dim, blocks in cuts:
        steps = jnp.exp(jax.random.uniform(jax.random.fold_in(own, dim), (blocks,), jnp.float32, smallest / len(cuts), top_value / len(cuts)))
        level = level * jnp.repeat(steps, shape[dim] // blocks).reshape([-1 if axis == dim else 1 for axis in range(len(shape))])
    return level


def bell_draw(rng, dims, deviation, most, split=(), dtype=jnp.bfloat16):
    gain = block_scale(rng, dims, split, -0.22, 0.18) if split else 1.0
    drawn = jax.random.normal(rng, dims, jnp.float32) * deviation * gain
    return jnp.minimum(jnp.maximum(drawn, -most), most).astype(dtype)


def setup_inputs(seed: int = 0, part: int = 0) -> dict:
    streams_of = jax.random.split(jax.random.key(seed), 6)
    couplings = bell_draw(streams_of[0], (9, NT, NZ, LY, LX, NC, 2 * NC), (18 * NC) ** -0.5, 0.15625, ((1, 4), (2, 4)), jnp.float32)
    source = bell_draw(streams_of[1], (NT, NZ, LY, LX, NC, 2 * NR), 1.0, 6.0, ((0, 4), (1, 4)), jnp.float32)
    initial = bell_draw(streams_of[2], (NT, NZ, LY, LX, NC, 2 * NR), 1.0, 6.0, ((0, 4), (1, 4)), jnp.float32)
    vectors = bell_draw(streams_of[3], (NV, NT, NZ, LY, LX, 2 * NC), (2 * NC * LX * LY * NZ * NT) ** -0.5, 0.0390625, ((1, 4), (2, 4)), jnp.float32)
    inverse_eigen = jnp.clip(jax.random.uniform(streams_of[4], (2, NV), jnp.float32, -20.0, 20.0), -20.0, 20.0)
    return {"couplings": couplings, "source": source, "initial": initial, "vectors": vectors, "inverse_eigen": inverse_eigen}


def coupled(matrix, spinor):
    middle = spinor.shape[-1] // 2
    turned = jnp.concatenate([-spinor[..., middle:], spinor[..., :middle]], axis=-1)
    stacked = jnp.concatenate([spinor, turned], axis=-2)
    return jnp.einsum("tzyxij,tzyxjn->tzyxin", matrix, stacked, precision=lax.Precision.HIGHEST)


def apply_operator(spinor, couplings):
    forward_t = jnp.roll(spinor, -1, 0)
    forward_t = forward_t.at[-1].multiply(-1.0)
    backward_t = jnp.roll(spinor, 1, 0)
    backward_t = backward_t.at[0].multiply(-1.0)
    neighbours = [spinor, jnp.roll(spinor, -1, 3), jnp.roll(spinor, 1, 3), jnp.roll(spinor, -1, 2), jnp.roll(spinor, 1, 2), jnp.roll(spinor, -1, 1), jnp.roll(spinor, 1, 1), forward_t, backward_t]
    summed = jnp.zeros_like(spinor)
    for direction in range(9):
        summed = summed + coupled(couplings[direction], neighbours[direction])
    return summed


def deflate(residual, vectors, inverse_eigen):
    middle = residual.shape[-1] // 2
    number = vectors.shape[0]
    negated = jnp.concatenate([residual[..., middle:], -residual[..., :middle]], axis=-1)
    stacked = jnp.concatenate([residual, negated], axis=-2)
    coefficients = jnp.dot(vectors.reshape(number, -1), stacked.reshape(-1, stacked.shape[-1]), precision=lax.Precision.HIGHEST, preferred_element_type=jnp.float32)
    eigen_real = inverse_eigen[0][:, None]
    eigen_imag = inverse_eigen[1][:, None]
    coef_real = coefficients[:, :middle]
    coef_imag = coefficients[:, middle:]
    scaled_real = eigen_real * coef_real - eigen_imag * coef_imag
    scaled_imag = eigen_real * coef_imag + eigen_imag * coef_real
    dstack = jnp.stack([jnp.concatenate([scaled_real, scaled_imag], axis=-1), jnp.concatenate([-scaled_imag, scaled_real], axis=-1)])
    halves = vectors.reshape(vectors.shape[:-1] + (2, vectors.shape[-1] // 2))
    return jnp.einsum("ktzyxci,ckn->tzyxin", halves, dstack, precision=lax.Precision.HIGHEST)


def reference(couplings, source, initial, vectors, inverse_eigen):
    iterate = initial
    residual = source
    for sweep in range(ITERS):
        residual = source - apply_operator(iterate, couplings)
        iterate = iterate + deflate(residual, vectors, inverse_eigen) + 0.5 * residual
    return iterate, residual
```

```python
import functools

import jax
import jax.numpy as jnp
from jax import lax
from jax.experimental import pallas as pl
from jax.experimental.pallas import tpu as pltpu
from jax.sharding import PartitionSpec as P

ITERS = 2
MESH = pl.DeviceIdType.MESH
F32 = jnp.float32
BF16 = jnp.bfloat16


def split(value):
    high = value.astype(BF16)
    low = (value - high.astype(F32)).astype(BF16)
    return high, low


def times_i(v):
    middle = v.shape[-1] // 2
    return jnp.concatenate([-v[:, middle:], v[:, :middle]], axis=1)


def times_minus_i(v):
    middle = v.shape[-1] // 2
    return jnp.concatenate([v[:, middle:], -v[:, :middle]], axis=1)


def dot(a, b):
    return jnp.dot(a, b, preferred_element_type=F32)


class Dims:
    def __init__(self, mesh, ly, lx, nc, width, nv):
        self.ns, self.nt = mesh.shape["space"], mesh.shape["tm"]
        self.ly, self.lx, self.nc, self.width, self.nv = ly, lx, nc, width, nv
        self.sites = ly * lx
        self.members = self.ns // 2 * self.nt
        self.half = nv // 2
        self.pieces = min(self.members, self.half // 8)
        self.rows = self.half // self.pieces


def kernel(
    D, coup_h, src_h, x0_h, vec_h, eig, sol, res,
    coup, src, x0, vec, x1, local_sem,
    m_self, m_halo, wk_hi, wk_lo, wt_hi, wt_lo, acc, dst_hi, dst_lo,
    halo, part, core_in, mine, rs_in, dfull,
    halo_send, halo_recv, core_send, core_recv, rs_send, rs_recv, ag_send, ag_recv, re_send, re_recv,
):
    ns, nt, sites, nc, lx, ly = D.ns, D.nt, D.sites, D.nc, D.lx, D.ly
    nv, half, rows, pieces, members = D.nv, D.half, D.rows, D.pieces, D.members
    me_s, me_t = lax.axis_index("space"), lax.axis_index("tm")
    parity = lax.rem(me_s, 2)
    pairs = ns // 2
    rank = me_t * pairs + me_s // 2
    partner = {"space": me_s + 1 - 2 * parity, "tm": me_t}

    loads = [
        pltpu.make_async_copy(x0_h, x0, local_sem.at[0]),
        pltpu.make_async_copy(coup_h, coup, local_sem.at[1]),
        pltpu.make_async_copy(vec_h, vec, local_sem.at[2]),
        pltpu.make_async_copy(src_h, src, local_sem.at[3]),
    ]
    for load in loads:
        load.start()

    barrier = pltpu.get_barrier_semaphore()
    total = ns * nt
    flat = me_t * ns + me_s

    def greet(o, carry):
        other = lax.rem(flat + o, total)
        pl.semaphore_signal(
            barrier, inc=1, device_id={"space": lax.rem(other, ns), "tm": other // ns}, device_id_type=MESH
        )
        return carry

    lax.fori_loop(1, total, greet, 0)
    pl.semaphore_wait(barrier, total - 1)

    up_s, down_s = lax.rem(me_s + 1, ns), lax.rem(me_s + ns - 1, ns)
    up_t, down_t = lax.rem(me_t + 1, nt), lax.rem(me_t + nt - 1, nt)
    targets = (
        (2, {"space": me_s, "tm": down_t}),
        (3, {"space": me_s, "tm": up_t}),
        (0, {"space": down_s, "tm": me_t}),
        (1, {"space": up_s, "tm": me_t}),
    )

    def halo_copy(it, site, slot, target):
        source = x0_h if it == 0 else x1
        return pltpu.make_async_remote_copy(
            src_ref=source.at[site],
            dst_ref=halo.at[it, slot, site],
            send_sem=halo_send.at[it, slot, site],
            recv_sem=halo_recv.at[it, slot, site],
            device_id=target,
            device_id_type=MESH,
        )

    def send_halo(it, first, count):
        def body(site, carry):
            for slot, target in targets:
                halo_copy(it, site, slot, target).start()
            return carry

        lax.fori_loop(first, first + count, body, 0)

    send_halo(0, 0, sites)
    sign_up = jnp.where(me_t == nt - 1, -1.0, 1.0).astype(F32)
    sign_down = jnp.where(me_t == 0, -1.0, 1.0).astype(F32)

    for load in loads:
        load.wait()

    def outs_of(site):
        y, x = site // lx, lax.rem(site, lx)
        return (
            site,
            y * lx + lax.rem(x + lx - 1, lx),
            y * lx + lax.rem(x + 1, lx),
            lax.rem(y + ly - 1, ly) * lx + x,
            lax.rem(y + 1, ly) * lx + x,
        )

    def prepare_matrices(site, carry):
        for d, out in enumerate(outs_of(site)):
            high, low = split(coup[d, out])
            m_self[site, d * nc:(d + 1) * nc, :] = high
            m_self[site, (5 + d) * nc:(6 + d) * nc, :] = low
        for d in range(4):
            high, low = split(coup[5 + d, site])
            m_halo[d, site, 0:nc, :] = high
            m_halo[d, site, nc:2 * nc, :] = low
        return carry

    lax.fori_loop(0, sites, prepare_matrices, 0)

    def stacked(value):
        high, low = split(value)
        return (
            jnp.concatenate([high, times_i(high)], axis=0),
            jnp.concatenate([low, times_i(low)], axis=0),
        )

    def self_part(field):
        acc[...] = jnp.zeros_like(acc)

        def body(site, carry):
            high, low = stacked(field[site])
            one = dot(m_self[site], high)
            two = dot(m_self[site, 0:5 * nc, :], low)
            for d, out in enumerate(outs_of(site)):
                acc[out] += (
                    one[d * nc:(d + 1) * nc] + one[(5 + d) * nc:(6 + d) * nc] + two[d * nc:(d + 1) * nc]
                )
            return carry

        lax.fori_loop(0, sites, body, 0)

    def prepare_vectors(site, carry):
        w = vec[site]
        high, low = split(w)
        wk_hi[site] = high
        wk_lo[site] = low
        turned = w.T
        high, low = split(turned)
        wt_hi[site, :, 0:nv] = high[0:nc]
        wt_hi[site, :, nv:2 * nv] = high[nc:2 * nc]
        wt_lo[site, :, 0:nv] = low[0:nc]
        wt_lo[site, :, nv:2 * nv] = low[nc:2 * nc]
        return carry

    def halo_part(it, out):
        def body(site, carry):
            total = acc[site]
            for slot, sign in ((0, None), (1, None), (2, sign_up), (3, sign_down)):
                copy = [t for t in targets if t[0] == slot][0]
                halo_copy(it, site, slot, copy[1]).wait_recv()
                value = halo[it, slot, site]
                if sign is not None:
                    value = value * sign
                high, low = stacked(value)
                one = dot(m_halo[slot, site], high)
                two = dot(m_halo[slot, site, 0:nc, :], low)
                total = total + (one[0:nc] + one[nc:2 * nc] + two)
            residual = src[site] - total
            out[site] = residual
            high, low = split(residual)
            high = jnp.concatenate([high, times_minus_i(high)], axis=0)
            low = jnp.concatenate([low, times_minus_i(low)], axis=0)
            part[it] += dot(wk_hi[site], high) + dot(wk_hi[site], low) + dot(wk_lo[site], high)
            return carry

        part[it] = jnp.zeros((nv, D.width), F32)
        lax.fori_loop(0, sites, body, 0)

    def member(q):
        return {"space": lax.rem(q, pairs) * 2 + parity, "tm": q // pairs}

    my_rows = pl.multiple_of(parity * half, 8)
    other_rows = pl.multiple_of((1 - parity) * half, 8)
    piece = lax.rem(rank, pieces)
    block = rank - piece
    piece_row = pl.multiple_of(my_rows + piece * rows, 8)

    def core_copy(it):
        return pltpu.make_async_remote_copy(
            src_ref=part.at[it, pl.ds(other_rows, half)],
            dst_ref=core_in.at[it],
            send_sem=core_send.at[it],
            recv_sem=core_recv.at[it],
            device_id=partner,
            device_id_type=MESH,
        )

    def rs_copy(it, o):
        q = lax.rem(rank + o, members)
        row = pl.multiple_of(lax.rem(q, pieces) * rows, 8)
        return pltpu.make_async_remote_copy(
            src_ref=mine.at[it, pl.ds(row, rows)],
            dst_ref=rs_in.at[it, o],
            send_sem=rs_send.at[it, o],
            recv_sem=rs_recv.at[it, o],
            device_id=member(q),
            device_id_type=MESH,
        )

    def ag_copy(it, o):
        q = block + lax.rem(piece + o, pieces)
        return pltpu.make_async_remote_copy(
            src_ref=dfull.at[it, pl.ds(piece_row, rows)],
            dst_ref=dfull.at[it, pl.ds(piece_row, rows)],
            send_sem=ag_send.at[it, o],
            recv_sem=ag_recv.at[it, o],
            device_id=member(q),
            device_id_type=MESH,
        )

    def relay_copy(it, o):
        row = pl.multiple_of(my_rows + lax.rem(piece + pieces - o, pieces) * rows, 8)
        return pltpu.make_async_remote_copy(
            src_ref=dfull.at[it, pl.ds(row, rows)],
            dst_ref=dfull.at[it, pl.ds(row, rows)],
            send_sem=re_send.at[it, o],
            recv_sem=re_recv.at[it, o],
            device_id=partner,
            device_id_type=MESH,
        )

    def loop(start, stop, action):
        def body(o, carry):
            action(o)
            return carry

        lax.fori_loop(start, stop, body, 0)

    def reduce_coefficients(it):
        core_copy(it).start()
        core_copy(it).wait_recv()
        mine[it] = part[it, pl.ds(my_rows, half), :] + core_in[it]
        loop(1, members, lambda o: rs_copy(it, o).start())
        own = mine[it, pl.ds(pl.multiple_of(piece * rows, 8), rows), :]

        def gather(o, total):
            rs_copy(it, o).wait_recv()
            return total + rs_in[it, o]

        coef = lax.fori_loop(1, members, gather, own)
        eigen = eig[pl.ds(piece_row, rows), :]
        dfull[it, pl.ds(piece_row, rows), :] = eigen[:, 0:1] * coef + eigen[:, 1:2] * times_i(coef)
        loop(1, pieces, lambda o: ag_copy(it, o).start())
        relay_copy(it, 0).start()

        def forward(o):
            ag_copy(it, o).wait_recv()
            relay_copy(it, o).start()

        loop(1, pieces, forward)
        loop(0, pieces, lambda o: relay_copy(it, o).wait_recv())
        high, low = split(dfull[it])
        dst_hi[0:nv, :] = high
        dst_hi[nv:2 * nv, :] = times_i(high)
        dst_lo[0:nv, :] = low
        dst_lo[nv:2 * nv, :] = times_i(low)

    def update(it, old, residual, out, group):
        def body(g, carry):
            first = g * group
            a_hi = wt_hi[pl.ds(first, group)].reshape(group * nc, 2 * nv)
            a_lo = wt_lo[pl.ds(first, group)].reshape(group * nc, 2 * nv)
            deflated = dot(a_hi, dst_hi[...]) + dot(a_hi, dst_lo[...]) + dot(a_lo, dst_hi[...])
            deflated = deflated.reshape(group, nc, D.width)
            now = pl.ds(first, group)
            out[now] = old[now] + deflated + 0.5 * residual[now]
            if it + 1 < ITERS:
                send_halo(it + 1, first, group)
            return carry

        lax.fori_loop(0, sites // group, body, 0)

    group = 4 if sites % 4 == 0 else 1
    self_part(x0)
    lax.fori_loop(0, sites, prepare_vectors, 0)
    halo_part(0, res)
    reduce_coefficients(0)
    update(0, x0, res, x1, group)
    self_part(x1)
    halo_part(1, res)
    reduce_coefficients(1)
    update(1, x1, res, sol, group)

    for it in range(ITERS):
        core_copy(it).wait_send()
        loop(1, members, lambda o: rs_copy(it, o).wait_send())
        loop(1, pieces, lambda o: ag_copy(it, o).wait_send())
        loop(0, pieces, lambda o: relay_copy(it, o).wait_send())

        def drain(site):
            for slot, target in targets:
                halo_copy(it, site, slot, target).wait_send()

        loop(0, sites, drain)


def solve(mesh, couplings, source, initial, vectors, inverse_eigen):
    nine, _, _, ly, lx, nc, _ = couplings.shape
    width = source.shape[-1]
    nv = vectors.shape[0]
    D = Dims(mesh, ly, lx, nc, width, nv)
    sites = D.sites
    field = (sites, nc, width)
    vecs = vectors.reshape(nv, sites, 2 * nc).transpose(1, 0, 2)
    any_spec = pl.BlockSpec(memory_space=pl.ANY)
    vmem = pl.BlockSpec(memory_space=pltpu.VMEM)
    dma = pltpu.SemaphoreType.DMA
    out = jax.ShapeDtypeStruct(field, F32)
    x, r = pl.pallas_call(
        functools.partial(kernel, D),
        out_shape=(out, out),
        in_specs=[any_spec, any_spec, any_spec, any_spec, vmem],
        out_specs=(vmem, vmem),
        scratch_shapes=[
            pltpu.VMEM((nine, sites, nc, 2 * nc), F32),
            pltpu.VMEM(field, F32),
            pltpu.VMEM(field, F32),
            pltpu.VMEM((sites, nv, 2 * nc), F32),
            pltpu.VMEM(field, F32),
            dma((4,)),
            pltpu.VMEM((sites, 10 * nc, 2 * nc), BF16),
            pltpu.VMEM((4, sites, 2 * nc, 2 * nc), BF16),
            pltpu.VMEM((sites, nv, 2 * nc), BF16),
            pltpu.VMEM((sites, nv, 2 * nc), BF16),
            pltpu.VMEM((sites, nc, 2 * nv), BF16),
            pltpu.VMEM((sites, nc, 2 * nv), BF16),
            pltpu.VMEM(field, F32),
            pltpu.VMEM((2 * nv, width), BF16),
            pltpu.VMEM((2 * nv, width), BF16),
            pltpu.VMEM((ITERS, 4) + field, F32),
            pltpu.VMEM((ITERS, nv, width), F32),
            pltpu.VMEM((ITERS, D.half, width), F32),
            pltpu.VMEM((ITERS, D.half, width), F32),
            pltpu.VMEM((ITERS, D.members, D.rows, width), F32),
            pltpu.VMEM((ITERS, nv, width), F32),
            dma((ITERS, 4, sites)),
            dma((ITERS, 4, sites)),
            dma((ITERS,)),
            dma((ITERS,)),
            dma((ITERS, D.members)),
            dma((ITERS, D.members)),
            dma((ITERS, D.pieces)),
            dma((ITERS, D.pieces)),
            dma((ITERS, D.pieces)),
            dma((ITERS, D.pieces)),
        ],
        compiler_params=pltpu.CompilerParams(
            collective_id=0, has_side_effects=True, vmem_limit_bytes=60 * 1024 * 1024
        ),
    )(
        couplings.reshape(nine, sites, nc, 2 * nc),
        source.reshape(field),
        initial.reshape(field),
        vecs,
        inverse_eigen.T,
    )
    return x.reshape(source.shape), r.reshape(source.shape)


def solution(mesh):
    in_specs = (
        P(None, "tm", "space", None, None, None, None),
        P("tm", "space", None, None, None, None),
        P("tm", "space", None, None, None, None),
        P(None, "tm", "space", None, None, None),
        P(),
    )
    out_specs = (
        P(("groups", "tm"), "space", None, None, None, None),
        P(("groups", "tm"), "space", None, None, None, None),
    )
    return jax.shard_map(
        functools.partial(solve, mesh), mesh=mesh, in_specs=in_specs, out_specs=out_specs, check_vma=False
    )
```

```python
import functools

import jax
import jax.numpy as jnp
from jax import lax
from jax.experimental import pallas as pl
from jax.experimental.pallas import tpu as pltpu
from jax.sharding import PartitionSpec as P

ITERS = 2
MESH = pl.DeviceIdType.MESH
F32 = jnp.float32
BF16 = jnp.bfloat16


def split(value):
    high = value.astype(BF16)
    low = (value - high.astype(F32)).astype(BF16)
    return high, low


def turn(v):
    middle = v.shape[-1] // 2
    lane = lax.broadcasted_iota(jnp.int32, v.shape, 1)
    return jnp.where(lane < middle, -1.0, 1.0) * pltpu.roll(v, middle, 1)


def dot(a, b):
    return jnp.dot(a, b, preferred_element_type=F32)


AHEAD = 3


class Dims:
    def __init__(self, mesh, ly, lx, nc, width, nv):
        self.ns, self.nt = mesh.shape["space"], mesh.shape["tm"]
        self.ly, self.lx, self.nc, self.width, self.nv = ly, lx, nc, width, nv
        self.chunks = 2
        self.cw = width // self.chunks
        self.phases = ITERS * self.chunks
        self.sites = ly * lx
        self.members = self.ns // 2 * self.nt
        self.half = nv // 2
        self.pieces = min(self.members, self.half // 8)
        self.rows = self.half // self.pieces


def kernel(
    D, coup_h, src_in, x0_in, vec_h, eig, sol, res_out,
    coup, vec, x0, src, x1, xf, res, local_sem,
    m_self, m_halo, wk_hi, wk_lo, wt_hi, wt_lo, acc, dst_hi, dst_lo,
    halo, part, core_in, mine, rs_in, dfull, eig_t,
    halo_send, halo_recv, core_send, core_recv, rs_send, rs_recv, ag_send, ag_recv, re_send, re_recv,
):
    ns, nt, sites, nc, lx, ly = D.ns, D.nt, D.sites, D.nc, D.lx, D.ly
    nv, half, rows, pieces, members = D.nv, D.half, D.rows, D.pieces, D.members
    chunks, cw, width = D.chunks, D.cw, D.width
    me_s, me_t = lax.axis_index("space"), lax.axis_index("tm")
    parity = lax.rem(me_s, 2)
    pairs = ns // 2
    rank = me_t * pairs + me_s // 2
    partner = {"space": me_s + 1 - 2 * parity, "tm": me_t}

    def loop(start, stop, action):
        def body(o, carry):
            action(o)
            return carry

        lax.fori_loop(start, stop, body, 0)

    loads = [
        pltpu.make_async_copy(coup_h, coup, local_sem.at[0]),
        pltpu.make_async_copy(vec_h, vec, local_sem.at[1]),
    ]
    for load in loads:
        load.start()

    barrier = pltpu.get_barrier_semaphore()
    total = ns * nt
    flat = me_t * ns + me_s

    def greet(o):
        other = lax.rem(flat + o, total)
        pl.semaphore_signal(
            barrier, inc=1, device_id={"space": lax.rem(other, ns), "tm": other // ns}, device_id_type=MESH
        )

    loop(1, total, greet)

    def pack(whole, parts):
        def body(site):
            value = whole[site]
            h, middle = cw // 2, width // 2
            for g in range(chunks):
                parts[g, site] = jnp.concatenate(
                    [value[:, g * h:(g + 1) * h], value[:, middle + g * h:middle + (g + 1) * h]], axis=1
                )

        loop(0, sites, body)

    def unpack(parts, whole):
        def body(site):
            h = cw // 2
            values = [parts[g, site] for g in range(chunks)]
            whole[site] = jnp.concatenate([v[:, :h] for v in values] + [v[:, h:] for v in values], axis=1)

        loop(0, sites, body)

    pack(x0_in, x0)
    pl.semaphore_wait(barrier, total - 1)

    up_s, down_s = lax.rem(me_s + 1, ns), lax.rem(me_s + ns - 1, ns)
    up_t, down_t = lax.rem(me_t + 1, nt), lax.rem(me_t + nt - 1, nt)
    targets = (
        (2, {"space": me_s, "tm": down_t}),
        (3, {"space": me_s, "tm": up_t}),
        (0, {"space": down_s, "tm": me_t}),
        (1, {"space": up_s, "tm": me_t}),
    )
    target_of = dict(targets)

    def field_of(p):
        return (x0 if p < chunks else x1).at[p % chunks]

    def halo_copy(p, site, slot):
        return pltpu.make_async_remote_copy(
            src_ref=field_of(p).at[site],
            dst_ref=halo.at[p, slot, site],
            send_sem=halo_send.at[p, slot, site],
            recv_sem=halo_recv.at[p, slot, site],
            device_id=target_of[slot],
            device_id_type=MESH,
        )

    def send_site(p, site):
        for slot, _ in targets:
            halo_copy(p, site, slot).start()

    loop(0, sites, lambda site: send_site(0, site))
    sign_up = jnp.where(me_t == nt - 1, -1.0, 1.0).astype(F32)
    sign_down = jnp.where(me_t == 0, -1.0, 1.0).astype(F32)

    pack(src_in, src)
    eig_t[...] = jnp.concatenate([eig[...]] * 4, axis=0).T
    for load in loads:
        load.wait()

    def outs_of(site):
        y, x = site // lx, lax.rem(site, lx)
        return (
            site,
            y * lx + lax.rem(x + lx - 1, lx),
            y * lx + lax.rem(x + 1, lx),
            lax.rem(y + ly - 1, ly) * lx + x,
            lax.rem(y + 1, ly) * lx + x,
        )

    def prepare_matrices(site):
        for d, out in enumerate(outs_of(site)):
            high, low = split(coup[d, out])
            m_self[site, d * nc:(d + 1) * nc, :] = high
            m_self[site, (5 + d) * nc:(6 + d) * nc, :] = low
        for d in range(4):
            high, low = split(coup[5 + d, site])
            m_halo[d, site, 0:nc, :] = high
            m_halo[d, site, nc:2 * nc, :] = low

    def prepare_vectors(site):
        turned = vec[site]
        high, low = split(turned.T)
        wk_hi[site] = high
        wk_lo[site] = low
        high, low = split(turned)
        wt_hi[site, :, 0:nv] = high[0:nc]
        wt_hi[site, :, nv:2 * nv] = high[nc:2 * nc]
        wt_lo[site, :, 0:nv] = low[0:nc]
        wt_lo[site, :, nv:2 * nv] = low[nc:2 * nc]

    def stacked(value, other):
        high, low = split(value)
        other_high, other_low = split(other)
        return jnp.concatenate([high, other_high], axis=0), jnp.concatenate([low, other_low], axis=0)

    def self_part(p):
        acc[...] = jnp.zeros_like(acc)
        field = field_of(p)

        def body(site):
            value = field[site]
            high, low = stacked(value, turn(value))
            one = dot(m_self[site], high)
            two = dot(m_self[site, 0:5 * nc, :], low)
            for d, out in enumerate(outs_of(site)):
                acc[out] += (
                    one[d * nc:(d + 1) * nc] + one[(5 + d) * nc:(6 + d) * nc] + two[d * nc:(d + 1) * nc]
                )

        loop(0, sites, body)
        part[p] = jnp.zeros((nv, cw), F32)

    def halo_site(p, site):
        g = p % chunks
        total = acc[site]
        for slot, sign in ((0, None), (1, None), (2, sign_up), (3, sign_down)):
            halo_copy(p, site, slot).wait_recv()
            value = halo[p, slot, site]
            if sign is not None:
                value = value * sign
            high, low = stacked(value, turn(value))
            one = dot(m_halo[slot, site], high)
            two = dot(m_halo[slot, site, 0:nc, :], low)
            total = total + (one[0:nc] + one[nc:2 * nc] + two)
        residual = src[g, site] - total
        res[g, site] = residual
        high, low = stacked(residual, -turn(residual))
        part[p] += dot(wk_hi[site], high) + dot(wk_hi[site], low) + dot(wk_lo[site], high)
        if p == 0:
            ahead = site + AHEAD - sites

            @pl.when(ahead >= 0)
            def _():
                send_site(1, ahead)
        else:
            @pl.when(site + AHEAD < sites)
            def _():
                send_site(p, site + AHEAD)

    def member(q):
        return {"space": lax.rem(q, pairs) * 2 + parity, "tm": q // pairs}

    my_rows = pl.multiple_of(parity * half, 8)
    other_rows = pl.multiple_of((1 - parity) * half, 8)
    piece = lax.rem(rank, pieces)
    block = rank - piece
    piece_row = pl.multiple_of(my_rows + piece * rows, 8)

    def core_copy(p):
        return pltpu.make_async_remote_copy(
            src_ref=part.at[p, pl.ds(other_rows, half)],
            dst_ref=core_in.at[p],
            send_sem=core_send.at[p],
            recv_sem=core_recv.at[p],
            device_id=partner,
            device_id_type=MESH,
        )

    def rs_copy(p, o):
        q = lax.rem(rank + o, members)
        row = pl.multiple_of(lax.rem(q, pieces) * rows, 8)
        return pltpu.make_async_remote_copy(
            src_ref=mine.at[p, pl.ds(row, rows)],
            dst_ref=rs_in.at[p, o],
            send_sem=rs_send.at[p, o],
            recv_sem=rs_recv.at[p, o],
            device_id=member(q),
            device_id_type=MESH,
        )

    def ag_copy(p, o):
        q = block + lax.rem(piece + o, pieces)
        return pltpu.make_async_remote_copy(
            src_ref=dfull.at[p, pl.ds(piece_row, rows)],
            dst_ref=dfull.at[p, pl.ds(piece_row, rows)],
            send_sem=ag_send.at[p, o],
            recv_sem=ag_recv.at[p, o],
            device_id=member(q),
            device_id_type=MESH,
        )

    def relay_copy(p, o):
        row = pl.multiple_of(my_rows + lax.rem(piece + pieces - o, pieces) * rows, 8)
        return pltpu.make_async_remote_copy(
            src_ref=dfull.at[p, pl.ds(row, rows)],
            dst_ref=dfull.at[p, pl.ds(row, rows)],
            send_sem=re_send.at[p, o],
            recv_sem=re_recv.at[p, o],
            device_id=partner,
            device_id_type=MESH,
        )

    def reduce_start(p):
        core_copy(p).wait_recv()
        mine[p] = part[p, pl.ds(my_rows, half), :] + core_in[p]
        loop(1, members, lambda o: rs_copy(p, o).start())

    def gather_start(p):
        own = mine[p, pl.ds(pl.multiple_of(piece * rows, 8), rows), :]

        def gather(o, total):
            rs_copy(p, o).wait_recv()
            return total + rs_in[p, o]

        coef = lax.fori_loop(1, members, gather, own)
        eigen = eig_t[pl.ds(piece_row, rows), :]
        dfull[p, pl.ds(piece_row, rows), :] = eigen[:, 0:1] * coef + eigen[:, 1:2] * turn(coef)
        loop(1, pieces, lambda o: ag_copy(p, o).start())
        relay_copy(p, 0).start()

    def forward(p):
        def action(o):
            ag_copy(p, o).wait_recv()
            relay_copy(p, o).start()

        loop(1, pieces, action)

    def update(p):
        loop(0, pieces, lambda o: relay_copy(p, o).wait_recv())
        d = dfull[p]
        high, low = stacked(d, turn(d))
        dst_hi[...] = high
        dst_lo[...] = low
        g, later = p % chunks, p + chunks
        old, new = (x0, x1) if p < chunks else (x1, xf)
        group = 4 if sites % 4 == 0 else 1

        def body(b):
            first = b * group
            a_hi = wt_hi[pl.ds(first, group)].reshape(group * nc, 2 * nv)
            a_lo = wt_lo[pl.ds(first, group)].reshape(group * nc, 2 * nv)
            deflated = dot(a_hi, dst_hi[...]) + dot(a_hi, dst_lo[...]) + dot(a_lo, dst_hi[...])
            deflated = deflated.reshape(group, nc, cw)
            now = pl.ds(first, group)
            new[g, now] = old[g, now] + deflated + 0.5 * res[g, now]
            if later < D.phases:
                @pl.when(b == 0)
                def _():
                    for site in range(AHEAD):
                        send_site(later, site)

        loop(0, sites // group, body)

    loop(0, sites, prepare_matrices)
    self_part(0)
    loop(0, sites, prepare_vectors)
    loop(0, sites, lambda site: halo_site(0, site))
    core_copy(0).start()
    cuts = (0, sites // 8, sites // 2, sites - sites // 8, sites)
    for p in range(1, D.phases):
        self_part(p)
        stages = (reduce_start, gather_start, forward, None)
        for stage, start, stop in zip(stages, cuts[:-1], cuts[1:]):
            loop(start, stop, lambda site: halo_site(p, site))
            if stage is not None:
                stage(p - 1)
            if stage is forward:
                update(p - 1)
        core_copy(p).start()
    last = D.phases - 1
    unpack(res, res_out)
    reduce_start(last)
    gather_start(last)
    forward(last)
    update(last)
    unpack(xf, sol)

    for p in range(D.phases):
        core_copy(p).wait_send()
        loop(1, members, lambda o: rs_copy(p, o).wait_send())
        loop(1, pieces, lambda o: ag_copy(p, o).wait_send())
        loop(0, pieces, lambda o: relay_copy(p, o).wait_send())

        def drain(site):
            for slot, _ in targets:
                halo_copy(p, site, slot).wait_send()

        loop(0, sites, drain)


def solve(mesh, couplings, source, initial, vectors, inverse_eigen):
    nine, _, _, ly, lx, nc, _ = couplings.shape
    width = source.shape[-1]
    nv = vectors.shape[0]
    D = Dims(mesh, ly, lx, nc, width, nv)
    sites, phases, cw = D.sites, D.phases, D.cw
    field = (sites, nc, width)
    chunked = (D.chunks, sites, nc, cw)
    vecs = vectors.reshape(nv, sites, 2 * nc).transpose(1, 2, 0)
    any_spec = pl.BlockSpec(memory_space=pl.ANY)
    vmem = pl.BlockSpec(memory_space=pltpu.VMEM)
    dma = pltpu.SemaphoreType.DMA
    out = jax.ShapeDtypeStruct(field, F32)
    x, r = pl.pallas_call(
        functools.partial(kernel, D),
        out_shape=(out, out),
        in_specs=[any_spec, vmem, vmem, any_spec, vmem],
        out_specs=(vmem, vmem),
        scratch_shapes=[
            pltpu.VMEM((nine, sites, nc, 2 * nc), F32),
            pltpu.VMEM((sites, 2 * nc, nv), F32),
            pltpu.VMEM(chunked, F32),
            pltpu.VMEM(chunked, F32),
            pltpu.VMEM(chunked, F32),
            pltpu.VMEM(chunked, F32),
            pltpu.VMEM(chunked, F32),
            dma((2,)),
            pltpu.VMEM((sites, 10 * nc, 2 * nc), BF16),
            pltpu.VMEM((4, sites, 2 * nc, 2 * nc), BF16),
            pltpu.VMEM((sites, nv, 2 * nc), BF16),
            pltpu.VMEM((sites, nv, 2 * nc), BF16),
            pltpu.VMEM((sites, nc, 2 * nv), BF16),
            pltpu.VMEM((sites, nc, 2 * nv), BF16),
            pltpu.VMEM((sites, nc, cw), F32),
            pltpu.VMEM((2 * nv, cw), BF16),
            pltpu.VMEM((2 * nv, cw), BF16),
            pltpu.VMEM((phases, 4, sites, nc, cw), F32),
            pltpu.VMEM((phases, nv, cw), F32),
            pltpu.VMEM((phases, D.half, cw), F32),
            pltpu.VMEM((phases, D.half, cw), F32),
            pltpu.VMEM((phases, D.members, D.rows, cw), F32),
            pltpu.VMEM((phases, nv, cw), F32),
            pltpu.VMEM((nv, 8), F32),
            dma((phases, 4, sites)),
            dma((phases, 4, sites)),
            dma((phases,)),
            dma((phases,)),
            dma((phases, D.members)),
            dma((phases, D.members)),
            dma((phases, D.pieces)),
            dma((phases, D.pieces)),
            dma((phases, D.pieces)),
            dma((phases, D.pieces)),
        ],
        compiler_params=pltpu.CompilerParams(
            collective_id=0, has_side_effects=True, vmem_limit_bytes=50000 * 1024
        ),
    )(
        couplings.reshape(nine, sites, nc, 2 * nc),
        source.reshape(field),
        initial.reshape(field),
        vecs,
        inverse_eigen,
    )
    return x.reshape(source.shape), r.reshape(source.shape)


def solution(mesh):
    in_specs = (
        P(None, "tm", "space", None, None, None, None),
        P("tm", "space", None, None, None, None),
        P("tm", "space", None, None, None, None),
        P(None, "tm", "space", None, None, None),
        P(),
    )
    out_specs = (
        P(("groups", "tm"), "space", None, None, None, None),
        P(("groups", "tm"), "space", None, None, None, None),
    )
    return jax.shard_map(
        functools.partial(solve, mesh), mesh=mesh, in_specs=in_specs, out_specs=out_specs, check_vma=False
    )
```

```python
import functools

import jax
import jax.numpy as jnp
from jax import lax
from jax.experimental import pallas as pl
from jax.experimental.pallas import tpu as pltpu
from jax.sharding import PartitionSpec as P

ITERS = 2
MESH = pl.DeviceIdType.MESH
F32 = jnp.float32
BF16 = jnp.bfloat16


def split(value):
    high = value.astype(BF16)
    low = (value - high.astype(F32)).astype(BF16)
    return high, low


def times_i(v):
    middle = v.shape[-1] // 2
    return jnp.concatenate([-v[:, middle:], v[:, :middle]], axis=1)


def times_minus_i(v):
    middle = v.shape[-1] // 2
    return jnp.concatenate([v[:, middle:], -v[:, :middle]], axis=1)


def dot(a, b):
    return jnp.dot(a, b, preferred_element_type=F32)


class Dims:
    def __init__(self, mesh, ly, lx, nc, width, nv):
        self.ns, self.nt = mesh.shape["space"], mesh.shape["tm"]
        self.ly, self.lx, self.nc, self.width, self.nv = ly, lx, nc, width, nv
        self.sites = ly * lx
        self.members = self.ns // 2 * self.nt
        self.half = nv // 2
        self.pieces = min(self.members, self.half // 8)
        self.rows = self.half // self.pieces


def kernel(
    D, coup_h, src_h, x0_h, vec_h, eig, sol, res,
    coup, src, x0, vec, x1, local_sem,
    m_self, m_halo, wk_hi, wk_lo, wt_hi, wt_lo, acc, dst_hi, dst_lo,
    halo, part, core_in, mine, rs_in, dfull, eig_t,
    halo_send, halo_recv, core_send, core_recv, rs_send, rs_recv, ag_send, ag_recv, re_send, re_recv,
):
    ns, nt, sites, nc, lx, ly = D.ns, D.nt, D.sites, D.nc, D.lx, D.ly
    nv, half, rows, pieces, members = D.nv, D.half, D.rows, D.pieces, D.members
    me_s, me_t = lax.axis_index("space"), lax.axis_index("tm")
    parity = lax.rem(me_s, 2)
    pairs = ns // 2
    rank = me_t * pairs + me_s // 2
    partner = {"space": me_s + 1 - 2 * parity, "tm": me_t}

    loads = [
        pltpu.make_async_copy(x0_h, x0, local_sem.at[0]),
        pltpu.make_async_copy(coup_h, coup, local_sem.at[1]),
        pltpu.make_async_copy(vec_h, vec, local_sem.at[2]),
        pltpu.make_async_copy(src_h, src, local_sem.at[3]),
    ]
    for load in loads:
        load.start()

    barrier = pltpu.get_barrier_semaphore()
    total = ns * nt
    flat = me_t * ns + me_s

    def greet(o, carry):
        other = lax.rem(flat + o, total)
        pl.semaphore_signal(
            barrier, inc=1, device_id={"space": lax.rem(other, ns), "tm": other // ns}, device_id_type=MESH
        )
        return carry

    lax.fori_loop(1, total, greet, 0)
    pl.semaphore_wait(barrier, total - 1)

    up_s, down_s = lax.rem(me_s + 1, ns), lax.rem(me_s + ns - 1, ns)
    up_t, down_t = lax.rem(me_t + 1, nt), lax.rem(me_t + nt - 1, nt)
    targets = (
        (2, {"space": me_s, "tm": down_t}),
        (3, {"space": me_s, "tm": up_t}),
        (0, {"space": down_s, "tm": me_t}),
        (1, {"space": up_s, "tm": me_t}),
    )

    def halo_copy(it, site, slot, target):
        source = x0_h if it == 0 else x1
        return pltpu.make_async_remote_copy(
            src_ref=source.at[site],
            dst_ref=halo.at[it, slot, site],
            send_sem=halo_send.at[it, slot, site],
            recv_sem=halo_recv.at[it, slot, site],
            device_id=target,
            device_id_type=MESH,
        )

    def send_halo(it, first, count):
        def body(site, carry):
            for slot, target in targets:
                halo_copy(it, site, slot, target).start()
            return carry

        lax.fori_loop(first, first + count, body, 0)

    send_halo(0, 0, sites)
    sign_up = jnp.where(me_t == nt - 1, -1.0, 1.0).astype(F32)
    sign_down = jnp.where(me_t == 0, -1.0, 1.0).astype(F32)

    for load in loads:
        load.wait()

    def outs_of(site):
        y, x = site // lx, lax.rem(site, lx)
        return (
            site,
            y * lx + lax.rem(x + lx - 1, lx),
            y * lx + lax.rem(x + 1, lx),
            lax.rem(y + ly - 1, ly) * lx + x,
            lax.rem(y + 1, ly) * lx + x,
        )

    def prepare_matrices(site, carry):
        for d, out in enumerate(outs_of(site)):
            high, low = split(coup[d, out])
            m_self[site, d * nc:(d + 1) * nc, :] = high
            m_self[site, (5 + d) * nc:(6 + d) * nc, :] = low
        for d in range(4):
            high, low = split(coup[5 + d, site])
            m_halo[d, site, 0:nc, :] = high
            m_halo[d, site, nc:2 * nc, :] = low
        return carry

    lax.fori_loop(0, sites, prepare_matrices, 0)

    def stacked(value):
        high, low = split(value)
        return (
            jnp.concatenate([high, times_i(high)], axis=0),
            jnp.concatenate([low, times_i(low)], axis=0),
        )

    def self_part(field):
        acc[...] = jnp.zeros_like(acc)

        def body(site, carry):
            high, low = stacked(field[site])
            one = dot(m_self[site], high)
            two = dot(m_self[site, 0:5 * nc, :], low)
            for d, out in enumerate(outs_of(site)):
                acc[out] += (
                    one[d * nc:(d + 1) * nc] + one[(5 + d) * nc:(6 + d) * nc] + two[d * nc:(d + 1) * nc]
                )
            return carry

        lax.fori_loop(0, sites, body, 0)

    def prepare_vectors(site, carry):
        turned = vec[site]
        high, low = split(turned.T)
        wk_hi[site] = high
        wk_lo[site] = low
        high, low = split(turned)
        wt_hi[site, :, 0:nv] = high[0:nc]
        wt_hi[site, :, nv:2 * nv] = high[nc:2 * nc]
        wt_lo[site, :, 0:nv] = low[0:nc]
        wt_lo[site, :, nv:2 * nv] = low[nc:2 * nc]
        return carry

    def halo_part(it, out):
        def body(site, carry):
            total = acc[site]
            for slot, sign in ((0, None), (1, None), (2, sign_up), (3, sign_down)):
                copy = [t for t in targets if t[0] == slot][0]
                halo_copy(it, site, slot, copy[1]).wait_recv()
                value = halo[it, slot, site]
                if sign is not None:
                    value = value * sign
                high, low = stacked(value)
                one = dot(m_halo[slot, site], high)
                two = dot(m_halo[slot, site, 0:nc, :], low)
                total = total + (one[0:nc] + one[nc:2 * nc] + two)
            residual = src[site] - total
            out[site] = residual
            high, low = split(residual)
            high = jnp.concatenate([high, times_minus_i(high)], axis=0)
            low = jnp.concatenate([low, times_minus_i(low)], axis=0)
            part[it] += dot(wk_hi[site], high) + dot(wk_hi[site], low) + dot(wk_lo[site], high)
            return carry

        part[it] = jnp.zeros((nv, D.width), F32)
        lax.fori_loop(0, sites, body, 0)

    def member(q):
        return {"space": lax.rem(q, pairs) * 2 + parity, "tm": q // pairs}

    my_rows = pl.multiple_of(parity * half, 8)
    other_rows = pl.multiple_of((1 - parity) * half, 8)
    piece = lax.rem(rank, pieces)
    block = rank - piece
    piece_row = pl.multiple_of(my_rows + piece * rows, 8)

    def core_copy(it):
        return pltpu.make_async_remote_copy(
            src_ref=part.at[it, pl.ds(other_rows, half)],
            dst_ref=core_in.at[it],
            send_sem=core_send.at[it],
            recv_sem=core_recv.at[it],
            device_id=partner,
            device_id_type=MESH,
        )

    def rs_copy(it, o):
        q = lax.rem(rank + o, members)
        row = pl.multiple_of(lax.rem(q, pieces) * rows, 8)
        return pltpu.make_async_remote_copy(
            src_ref=mine.at[it, pl.ds(row, rows)],
            dst_ref=rs_in.at[it, o],
            send_sem=rs_send.at[it, o],
            recv_sem=rs_recv.at[it, o],
            device_id=member(q),
            device_id_type=MESH,
        )

    def ag_copy(it, o):
        q = block + lax.rem(piece + o, pieces)
        return pltpu.make_async_remote_copy(
            src_ref=dfull.at[it, pl.ds(piece_row, rows)],
            dst_ref=dfull.at[it, pl.ds(piece_row, rows)],
            send_sem=ag_send.at[it, o],
            recv_sem=ag_recv.at[it, o],
            device_id=member(q),
            device_id_type=MESH,
        )

    def relay_copy(it, o):
        row = pl.multiple_of(my_rows + lax.rem(piece + pieces - o, pieces) * rows, 8)
        return pltpu.make_async_remote_copy(
            src_ref=dfull.at[it, pl.ds(row, rows)],
            dst_ref=dfull.at[it, pl.ds(row, rows)],
            send_sem=re_send.at[it, o],
            recv_sem=re_recv.at[it, o],
            device_id=partner,
            device_id_type=MESH,
        )

    def loop(start, stop, action):
        def body(o, carry):
            action(o)
            return carry

        lax.fori_loop(start, stop, body, 0)

    def reduce_coefficients(it):
        core_copy(it).start()
        core_copy(it).wait_recv()
        mine[it] = part[it, pl.ds(my_rows, half), :] + core_in[it]
        loop(1, members, lambda o: rs_copy(it, o).start())
        own = mine[it, pl.ds(pl.multiple_of(piece * rows, 8), rows), :]

        def gather(o, total):
            rs_copy(it, o).wait_recv()
            return total + rs_in[it, o]

        coef = lax.fori_loop(1, members, gather, own)
        eigen = eig_t[pl.ds(piece_row, rows), :]
        dfull[it, pl.ds(piece_row, rows), :] = eigen[:, 0:1] * coef + eigen[:, 1:2] * times_i(coef)
        loop(1, pieces, lambda o: ag_copy(it, o).start())
        relay_copy(it, 0).start()

        def forward(o):
            ag_copy(it, o).wait_recv()
            relay_copy(it, o).start()

        loop(1, pieces, forward)
        loop(0, pieces, lambda o: relay_copy(it, o).wait_recv())
        high, low = split(dfull[it])
        dst_hi[0:nv, :] = high
        dst_hi[nv:2 * nv, :] = times_i(high)
        dst_lo[0:nv, :] = low
        dst_lo[nv:2 * nv, :] = times_i(low)

    def update(it, old, residual, out, group):
        def body(g, carry):
            first = g * group
            a_hi = wt_hi[pl.ds(first, group)].reshape(group * nc, 2 * nv)
            a_lo = wt_lo[pl.ds(first, group)].reshape(group * nc, 2 * nv)
            deflated = dot(a_hi, dst_hi[...]) + dot(a_hi, dst_lo[...]) + dot(a_lo, dst_hi[...])
            deflated = deflated.reshape(group, nc, D.width)
            now = pl.ds(first, group)
            out[now] = old[now] + deflated + 0.5 * residual[now]
            if it + 1 < ITERS:
                send_halo(it + 1, first, group)
            return carry

        lax.fori_loop(0, sites // group, body, 0)

    group = 4 if sites % 4 == 0 else 1
    self_part(x0)
    lax.fori_loop(0, sites, prepare_vectors, 0)
    eig_t[...] = jnp.concatenate([eig[...]] * 4, axis=0).T
    halo_part(0, res)
    reduce_coefficients(0)
    update(0, x0, res, x1, group)
    self_part(x1)
    halo_part(1, res)
    reduce_coefficients(1)
    update(1, x1, res, sol, group)

    for it in range(ITERS):
        core_copy(it).wait_send()
        loop(1, members, lambda o: rs_copy(it, o).wait_send())
        loop(1, pieces, lambda o: ag_copy(it, o).wait_send())
        loop(0, pieces, lambda o: relay_copy(it, o).wait_send())

        def drain(site):
            for slot, target in targets:
                halo_copy(it, site, slot, target).wait_send()

        loop(0, sites, drain)


def solve(mesh, couplings, source, initial, vectors, inverse_eigen):
    nine, _, _, ly, lx, nc, _ = couplings.shape
    width = source.shape[-1]
    nv = vectors.shape[0]
    D = Dims(mesh, ly, lx, nc, width, nv)
    sites = D.sites
    field = (sites, nc, width)
    vecs = vectors.reshape(nv, sites, 2 * nc).transpose(1, 2, 0)
    any_spec = pl.BlockSpec(memory_space=pl.ANY)
    vmem = pl.BlockSpec(memory_space=pltpu.VMEM)
    dma = pltpu.SemaphoreType.DMA
    out = jax.ShapeDtypeStruct(field, F32)
    x, r = pl.pallas_call(
        functools.partial(kernel, D),
        out_shape=(out, out),
        in_specs=[any_spec, any_spec, any_spec, any_spec, vmem],
        out_specs=(vmem, vmem),
        scratch_shapes=[
            pltpu.VMEM((nine, sites, nc, 2 * nc), F32),
            pltpu.VMEM(field, F32),
            pltpu.VMEM(field, F32),
            pltpu.VMEM((sites, 2 * nc, nv), F32),
            pltpu.VMEM(field, F32),
            dma((4,)),
            pltpu.VMEM((sites, 10 * nc, 2 * nc), BF16),
            pltpu.VMEM((4, sites, 2 * nc, 2 * nc), BF16),
            pltpu.VMEM((sites, nv, 2 * nc), BF16),
            pltpu.VMEM((sites, nv, 2 * nc), BF16),
            pltpu.VMEM((sites, nc, 2 * nv), BF16),
            pltpu.VMEM((sites, nc, 2 * nv), BF16),
            pltpu.VMEM(field, F32),
            pltpu.VMEM((2 * nv, width), BF16),
            pltpu.VMEM((2 * nv, width), BF16),
            pltpu.VMEM((ITERS, 4) + field, F32),
            pltpu.VMEM((ITERS, nv, width), F32),
            pltpu.VMEM((ITERS, D.half, width), F32),
            pltpu.VMEM((ITERS, D.half, width), F32),
            pltpu.VMEM((ITERS, D.members, D.rows, width), F32),
            pltpu.VMEM((ITERS, nv, width), F32),
            pltpu.VMEM((nv, 8), F32),
            dma((ITERS, 4, sites)),
            dma((ITERS, 4, sites)),
            dma((ITERS,)),
            dma((ITERS,)),
            dma((ITERS, D.members)),
            dma((ITERS, D.members)),
            dma((ITERS, D.pieces)),
            dma((ITERS, D.pieces)),
            dma((ITERS, D.pieces)),
            dma((ITERS, D.pieces)),
        ],
        compiler_params=pltpu.CompilerParams(
            collective_id=0, has_side_effects=True, vmem_limit_bytes=50000 * 1024
        ),
    )(
        couplings.reshape(nine, sites, nc, 2 * nc),
        source.reshape(field),
        initial.reshape(field),
        vecs,
        inverse_eigen,
    )
    return x.reshape(source.shape), r.reshape(source.shape)


def solution(mesh):
    in_specs = (
        P(None, "tm", "space", None, None, None, None),
        P("tm", "space", None, None, None, None),
        P("tm", "space", None, None, None, None),
        P(None, "tm", "space", None, None, None),
        P(),
    )
    out_specs = (
        P(("groups", "tm"), "space", None, None, None, None),
        P(("groups", "tm"), "space", None, None, None, None),
    )
    return jax.shard_map(
        functools.partial(solve, mesh), mesh=mesh, in_specs=in_specs, out_specs=out_specs, check_vma=False
    )
```
